256 devices in a mesh: req: 16 (over z, core), mp: 16 (over x, y).
Axes of the slice: x: 4, y: 4, z: 8, core: 2. Of those that a mesh axis runs over, the one named last changes fastest.
Arguments:
- tokens_in: bfloat16 [2048, 2048], P('req', 'mp'), may hold values from -6 to 6
- req_lengths: int32 [16, 4], replicated, may hold values from 1 to 64, 128 in all within a row
- req_groups: int32 [16, 4], replicated, may hold values from 0 to 1
- prefix_cache: bfloat16 [2, 4096, 2, 2048], P(None, 'req', None, 'mp'), may hold values from -170 to 170, as said below
- attn_gain: bfloat16 [2048], replicated, may hold values from 0.25 to 1.75
- mlp_gain: bfloat16 [2048], replicated, may hold values from 0.25 to 1.75
- w_qkv: bfloat16 [2048, 3, 2048], P(None, None, 'mp'), may hold values from -0.25 to 0.25
- w_out: bfloat16 [2048, 2048], P('mp'), may hold values from -0.1875 to 0.1875
- w_gate_up: bfloat16 [2048, 2, 5632], P(None, None, 'mp'), may hold values from -0.125 to 0.125
- w_down: bfloat16 [5632, 2048], P('mp'), may hold values from -0.109375 to 0.109375
Outputs:
- layer_out: bfloat16 [2048, 2048], P('req', 'mp')
The draws below stay inside these ranges and needn't reach their ends.
Inputs may be any that keep to these rules, and one draw needn't show every extreme that they name: `req_lengths`: in each row the 4 lengths sum to 128, and the largest is 64. `prefix_cache`: keys are cached after rotation.
All inputs are finite; a program needn't handle non-finite values.
Results may differ from the reference program's by a relative error of at most 0.02.
The reference program's roundings to bfloat16 on the way (of `normed_attn`, `query_rot`, `prefix_parts`, `attn_rows`, `residual`, `normed_mlp` and `hidden`) count: a program that leaves them out, or rounds other values in their place, can miss the bound.
Values may be sent and summed in bfloat16 or wider, within the bound.
A program may use at most 64 MiB of HBM per device.

```python
import functools
import math
import jax
import jax.numpy as jnp
import numpy as np
from jax import lax

D = 2048
HEADS = 32
HEAD_DIM = 64
FF = 5632
ROT = 16
PREFIX = 4096
GROUPS = 2
REQ_DEV = 4
TOK_DEV = 128
TOKENS = 2048
N_REQ = 16
N_MP = 16


def draw_prefix_cache(key, part):
    key_keys, key_values = jax.random.split(jax.random.fold_in(key, 11), 2)
    shape = (GROUPS, PREFIX, 1, D)
    keys_part = jnp.clip(2.0 * jax.random.normal(key_keys, shape, jnp.float32), -12.0, 12.0)
    values_part = jnp.clip(2.0 * jax.random.normal(key_values, shape, jnp.float32), -12.0, 12.0)
    return jnp.concatenate([keys_part, values_part], axis=2).astype(jnp.bfloat16)


def touch_ends(array, key, smallest, high):
    dims = array.shape
    place = [jax.random.randint(jax.random.fold_in(key, axis), (), 0, dims[axis]) for axis in range(len(dims))]
    array = array.at[tuple(place)].set(smallest)
    longest = dims.index(max(dims))
    place[longest] = (place[longest] + 1) % dims[longest]
    return array.at[tuple(place)].set(high)


def with_spikes(values, rng, source, target, blocks, factor):
    owner, partner = [(jnp.arange(values.shape[position]) // (values.shape[position] // blocks)).reshape([-1 if axis == position else 1 for axis in range(values.ndim)]) for position in (source, target)]
    chosen = jax.random.permutation(rng, blocks)[partner]
    strong = (owner == chosen) | (owner == (partner + blocks // 2) % blocks)
    return jnp.where(strong, factor * values, values)


def levels(stream_key, shape, cuts, least, high):
    level = 1.0
    for dim, shards_of in cuts:
        draws = jax.random.uniform(jax.random.fold_in(jax.random.fold_in(stream_key, 6), dim), (shards_of,), jnp.float32, least / len(cuts), high / len(cuts))
        level = level * jnp.repeat(jnp.exp(draws), shape[dim] // shards_of).reshape((-1,) + (1,) * (len(shape) - 1 - dim))
    return level


def split_up(amount, total, most, lean):
    loads = [(1 << 20) // math.isqrt(rank ** lean) + 1 for rank in range(2, amount + 1)]
    spare, given = total - most - (amount - 1), [1] * (amount - 1)
    while spare > 0:
        candidates = [i for i in range(amount - 1) if given[i] < most]
        mass, remaining = sum([loads[i] for i in candidates]), spare
        for i in candidates:
            more = min(most - given[i], max(1, remaining * loads[i] // mass), spare)
            given[i] = given[i] + more
            spare = spare - more
    return np.array([most] + given)


def ragged(rng, count, total, bound, lean):
    if count == 2:
        one = jax.random.randint(rng, (), max(1, total - bound), min(bound, total - 1) + 1)
        return jnp.stack([one, total - one])
    tallies = jnp.asarray(split_up(count, total, bound, lean), jnp.int32)
    twos = (count - 1) // 2
    giver, receiver = tallies[1:1 + 2 * twos:2], tallies[2:2 + 2 * twos:2]
    room = jnp.minimum(giver - 1, bound - receiver)
    moved = jax.random.randint(jax.random.fold_in(rng, 1), (twos,), 0, 1 << 20) % (room + 1)
    tallies = tallies.at[1:1 + 2 * twos:2].set(giver - moved).at[2:2 + 2 * twos:2].set(receiver + moved)
    return tallies[jax.random.permutation(jax.random.fold_in(rng, 2), count)]


def scatter_about(own_key, shape, scale, reach, cuts=(), held_as=jnp.bfloat16):
    values = jax.random.normal(own_key, shape, jnp.float32) * scale
    if len(cuts) > 0:
        values = levels(own_key, shape, cuts, -0.22, 0.18) * values
    return jnp.clip(values, min=-reach, max=reach).astype(held_as)


def gaussian_with(key, dims, scale, reach, cuts, heavy, kind=jnp.bfloat16):
    values = scale * jax.random.normal(key, dims, jnp.float32)
    if cuts:
        values = values * levels(key, dims, cuts, -0.22, 0.18)
    return jnp.clip(with_spikes(values, jax.random.fold_in(key, 3), *heavy), -reach, reach).astype(kind)


def setup_inputs(seed: int = 0) -> dict:
    arg_keys = jax.random.split(jax.random.key(seed), 11)
    return {
        "tokens_in": scatter_about(arg_keys[0], (TOKENS, D), 1.0, 6.0, ((0, 16), (1, 16))),
        "req_lengths": jax.vmap(lambda own: ragged(own, REQ_DEV, TOK_DEV, TOK_DEV // 2, 2))(jax.random.split(arg_keys[1], N_REQ)).reshape((N_REQ, REQ_DEV)).astype(jnp.int32),
        "req_groups": touch_ends(jax.random.randint(arg_keys[2], (N_REQ, REQ_DEV), 0, GROUPS), jax.random.fold_in(arg_keys[2], 1), 0, GROUPS - 1).astype(jnp.int32),
        "prefix_cache": draw_prefix_cache(jax.random.fold_in(arg_keys[10], 71), 0),
        "attn_gain": jnp.clip(1.0 + 0.15 * jax.random.normal(arg_keys[4], (D,), jnp.float32), 0.25, 1.75).astype(jnp.bfloat16),
        "mlp_gain": jnp.clip(1.0 + 0.15 * jax.random.normal(arg_keys[5], (D,), jnp.float32), 0.25, 1.75).astype(jnp.bfloat16),
        "w_qkv": scatter_about(arg_keys[6], (D, 3, D), (D // 4) ** -0.5, 0.25, ((2, 16),)),
        "w_out": gaussian_with(arg_keys[7], (D, D), D ** -0.5, 0.1875, ((0, 16),), (0, 1, 16, 2.0)),
        "w_gate_up": scatter_about(arg_keys[8], (D, 2, FF), D ** -0.5, 0.125, ((2, 16),)),
        "w_down": gaussian_with(arg_keys[9], (FF, D), FF ** -0.5, 0.109375, ((0, 16),), (0, 1, 16, 2.0)),
    }


NEG = -1e+30
EPS = 1e-05

def layer_norm(rows_in, gain_vec):
    values_f = rows_in.astype(jnp.float32)
    row_mean = lax.optimization_barrier(jnp.mean(values_f, axis=-1, keepdims=True))
    centred = values_f - row_mean
    variance = lax.optimization_barrier(jnp.mean(centred * centred, axis=-1, keepdims=True))
    return (centred * lax.rsqrt(variance + EPS) * gain_vec.astype(jnp.float32)).astype(jnp.bfloat16)

def rotary(vectors, positions):
    half_rot = ROT // 2
    frequency = 10000.0 ** (-(jnp.arange(half_rot, dtype=jnp.float32) * 2.0 / ROT))
    angles = positions[:, None] * frequency[None, :]
    cosine = jnp.cos(angles)[:, None, :]
    sine_part = jnp.sin(angles)[:, None, :]
    lower_half = vectors[..., :half_rot]
    upper_half = vectors[..., half_rot:ROT]
    return jnp.concatenate([lower_half * cosine - upper_half * sine_part, upper_half * cosine + lower_half * sine_part, vectors[..., ROT:]], axis=-1)

def token_meta(length_row, group_row, row_count):
    starts = jnp.cumsum(length_row) - length_row
    places = jnp.arange(row_count, dtype=jnp.int32)
    request = lax.optimization_barrier(jnp.sum((places[:, None] >= starts[None, :]).astype(jnp.int32), axis=1)) - 1
    onehot = (request[:, None] == jnp.arange(length_row.shape[0], dtype=jnp.int32)[None, :]).astype(jnp.int32)
    offset = places - lax.optimization_barrier(jnp.sum(onehot * starts[None, :], axis=1))
    groups_of = lax.optimization_barrier(jnp.sum(onehot * group_row[None, :], axis=1))
    return (request, offset, groups_of)

def rounded_sum(left, right, pieces):
    width = left.shape[1] // pieces

    def add_piece(running, index):
        left_part = lax.dynamic_slice_in_dim(left, index * width, width, 1)
        right_part = lax.dynamic_slice_in_dim(right, index * width, width, 0)
        term = jnp.dot(left_part, right_part, preferred_element_type=jnp.float32).astype(jnp.bfloat16)
        term = lax.optimization_barrier(term).astype(jnp.float32)
        return (running + term, None)
    start_sum = jnp.zeros((left.shape[0], right.shape[1]), jnp.float32)
    result, _ = lax.scan(add_piece, start_sum, jnp.arange(pieces, dtype=jnp.int32))
    return result

def reference(tokens_in, req_lengths, req_groups, prefix_cache, attn_gain, mlp_gain, w_qkv, w_out, w_gate_up, w_down):
    normed_attn = layer_norm(tokens_in, attn_gain)
    projected = jnp.dot(normed_attn, w_qkv.reshape(D, 3 * D), preferred_element_type=jnp.float32)
    projected = projected.reshape(TOKENS, 3, HEADS, HEAD_DIM)
    request, offset, groups_of = jax.vmap(functools.partial(token_meta, row_count=TOK_DEV))(req_lengths, req_groups)
    positions = (PREFIX + offset.reshape(TOKENS)).astype(jnp.float32)
    query_rot = rotary(projected[:, 0], positions).astype(jnp.bfloat16)
    key_rot = rotary(projected[:, 1], positions).astype(jnp.bfloat16)
    value_rows = projected[:, 2].astype(jnp.bfloat16)
    block_count = N_REQ
    prefix_rows = PREFIX // N_REQ
    prefix_keys = prefix_cache[:, :, 0].reshape(GROUPS, block_count, prefix_rows, HEADS, HEAD_DIM).astype(jnp.float32)
    prefix_values = prefix_cache[:, :, 1].reshape(GROUPS, block_count, prefix_rows, HEADS, HEAD_DIM).astype(jnp.float32)
    score_scale = HEAD_DIM ** (-0.5)

    def attend(inputs):
        block_query, block_keys, block_values, block_request, block_offset, block_groups = inputs
        query_f = block_query.astype(jnp.float32)
        pre_scores = jnp.einsum('thd,gbphd->htgbp', query_f, prefix_keys) * score_scale
        member = block_groups[:, None] == jnp.arange(GROUPS, dtype=jnp.int32)[None, :]
        pre_scores = jnp.where(member[None, :, :, None, None], pre_scores, NEG)
        block_top = lax.optimization_barrier(jnp.max(pre_scores, axis=(2, 4)))
        block_weights = jnp.exp(pre_scores - block_top[:, :, None, :, None])
        block_sum = lax.optimization_barrier(jnp.sum(block_weights, axis=(2, 4)))
        block_mixed = jnp.einsum('htgbp,gbphe->bthe', block_weights.astype(jnp.bfloat16).astype(jnp.float32), prefix_values)
        prefix_parts = (block_mixed / jnp.transpose(block_sum, (2, 1, 0))[..., None]).astype(jnp.bfloat16)
        own_scores = jnp.einsum('thd,shd->hts', query_f, block_keys.astype(jnp.float32)) * score_scale
        allowed = (block_request[:, None] == block_request[None, :]) & (block_offset[None, :] <= block_offset[:, None])
        own_scores = jnp.where(allowed[None], own_scores, NEG)
        own_top = lax.optimization_barrier(jnp.max(own_scores, axis=2))
        own_weights = jnp.exp(own_scores - own_top[:, :, None])
        own_sum = lax.optimization_barrier(jnp.sum(own_weights, axis=2))
        own_mixed = jnp.einsum('hts,she->the', own_weights.astype(jnp.bfloat16).astype(jnp.float32), block_values.astype(jnp.float32))
        top_all = jnp.maximum(own_top, lax.optimization_barrier(jnp.max(block_top, axis=2)))
        own_scale = jnp.exp(own_top - top_all)
        part_scale = block_sum * jnp.exp(block_top - top_all[:, :, None])
        numer = own_mixed * own_scale.T[:, :, None] + lax.optimization_barrier(jnp.sum(prefix_parts.astype(jnp.float32) * jnp.transpose(part_scale, (2, 1, 0))[..., None], axis=0))
        denom = own_sum * own_scale + lax.optimization_barrier(jnp.sum(part_scale, axis=2))
        return (numer / denom.T[:, :, None]).astype(jnp.bfloat16)
    attn_rows = lax.map(attend, (query_rot.reshape(N_REQ, TOK_DEV, HEADS, HEAD_DIM), key_rot.reshape(N_REQ, TOK_DEV, HEADS, HEAD_DIM), value_rows.reshape(N_REQ, TOK_DEV, HEADS, HEAD_DIM), request, offset, groups_of))
    attn_rows = attn_rows.reshape(TOKENS, D)
    attn_sum = rounded_sum(attn_rows, w_out, N_MP)
    residual = (tokens_in.astype(jnp.float32) + attn_sum).astype(jnp.bfloat16)
    normed_mlp = layer_norm(residual, mlp_gain)
    gate_up = jnp.dot(normed_mlp, w_gate_up.reshape(D, 2 * FF), preferred_element_type=jnp.float32).reshape(TOKENS, 2, FF)
    hidden = (jax.nn.silu(gate_up[:, 0]) * gate_up[:, 1]).astype(jnp.bfloat16)
    mlp_sum = rounded_sum(hidden, w_down, N_MP)
    return (residual.astype(jnp.float32) + mlp_sum).astype(jnp.bfloat16)
```

```python
import functools

import jax
import jax.numpy as jnp
from jax import lax
from jax.experimental import pallas as pl
from jax.experimental.pallas import tpu as pltpu
from jax.sharding import PartitionSpec as P

HEAD_DIM = 64
ROT = 16
PREFIX = 4096
NEG = -1e30
EPS = 1e-05
F32 = jnp.float32
BF16 = jnp.bfloat16
N_MP = 16
N_Z = 8
SIDE = 4
OFFSETS = sorted(
    [(dx, dy) for dx in range(SIDE) for dy in range(SIDE) if (dx, dy) != (0, 0)],
    key=lambda o: (-(min(o[0], SIDE - o[0]) + min(o[1], SIDE - o[1])), o),
)


def dot(a, b, dims=((1,), (0,))):
    return lax.dot_general(a, b, (dims, ((), ())), preferred_element_type=F32)


def layer_kernel(
    lengths, groups, tokens_hbm, prefix_hbm, gain_a_hbm, gain_m_hbm, wqkv_hbm, wout_hbm, wgu_hbm, wdown_hbm,
    out_ref,
    tok, pre, gain_a, gain_m, wqkv, wout, wgu, wdown,
    xf, kv, nrm, p1s, p1r, res, rf, p2s, p2r, q2, acc,
    local_sem, ag1_s, ag1_r, rs1_s, rs1_r, ag2_s, ag2_r, rs2_s, rs2_r, ring_s, ring_r, pair_s, pair_r,
):
    mp = lax.axis_index("mp")
    req = lax.axis_index("req")
    z, core = req // 2, req % 2
    mx, my = mp // SIDE, mp % SIDE

    def at_z(step):
        return lax.rem(z + (step + N_Z), N_Z) * 2 + core

    peers = [lax.rem(mx + dx, SIDE) * SIDE + lax.rem(my + dy, SIDE) for dx, dy in OFFSETS]
    sources = [
        lax.rem(mx + SIDE - dx, SIDE) * SIDE + lax.rem(my + SIDE - dy, SIDE) for dx, dy in OFFSETS
    ]
    right, left, partner = at_z(1), at_z(-1), z * 2 + (1 - core)

    barrier = pltpu.get_barrier_semaphore()
    for near in (right, left, partner):
        pl.semaphore_signal(barrier, inc=1, device_id={"req": near})
    for peer in peers:
        pl.semaphore_signal(barrier, inc=1, device_id={"mp": peer})

    def fetch(index, src, dst):
        copy = pltpu.make_async_copy(src, dst, local_sem.at[index])
        copy.start()
        return copy

    get_pre = fetch(0, prefix_hbm, pre)
    get_tok = fetch(1, tokens_hbm, tok)
    get_ga = fetch(2, gain_a_hbm, gain_a)
    get_gm = fetch(3, gain_m_hbm, gain_m)
    get_qkv = [
        fetch(4 + i, wqkv_hbm.at[i], wqkv.at[:, pl.ds(i * 128, 128)]) for i in range(3)
    ]
    get_out = fetch(7, wout_hbm, wout)
    get_gu = fetch(8, wgu_hbm, wgu)
    get_down = fetch(9, wdown_hbm, wdown)

    rows = kv.shape[2]
    get_pre.wait()
    pick_key = (
        lax.broadcasted_iota(jnp.int32, (2 * rows, rows), 0)
        == 2 * lax.broadcasted_iota(jnp.int32, (2 * rows, rows), 1)
    ).astype(F32).astype(BF16)
    pick_value = (
        lax.broadcasted_iota(jnp.int32, (rows, 2 * rows), 1)
        == 2 * lax.broadcasted_iota(jnp.int32, (rows, 2 * rows), 0) + 1
    ).astype(F32).astype(BF16)
    for g in range(2):
        raw = pre[pl.ds(g * 2 * rows, 2 * rows), :]
        kv[req, 0, pl.ds(g * 128, 128), :] = dot(raw, pick_key, ((0,), (0,))).astype(BF16)
        kv[req, 1, :, pl.ds(g * 128, 128)] = dot(pick_value, raw).astype(BF16)
    get_tok.wait()
    xf[mp] = tok[...]

    pl.semaphore_wait(barrier, 3 + len(OFFSETS))

    def ring_copy(way, hop, part):
        slot = at_z(-hop) if way == 0 else at_z(hop)
        index = way * 8 + hop * 2 + part
        return pltpu.make_async_remote_copy(
            src_ref=kv.at[slot, part], dst_ref=kv.at[slot, part],
            send_sem=ring_s.at[index], recv_sem=ring_r.at[index],
            device_id={"req": right if way == 0 else left},
        )

    def ring_landed(way, hop, part):
        slot = at_z(-hop) if way == 0 else at_z(hop)
        index = way * 8 + (hop - 1) * 2 + part
        return pltpu.make_async_remote_copy(
            src_ref=kv.at[slot, part], dst_ref=kv.at[slot, part],
            send_sem=ring_s.at[index], recv_sem=ring_r.at[index],
            device_id={"req": right if way == 0 else left},
        )

    def pair_copy(pos, slot, part):
        index = pos * 2 + part
        return pltpu.make_async_remote_copy(
            src_ref=kv.at[slot, part], dst_ref=kv.at[slot, part],
            send_sem=pair_s.at[index], recv_sem=pair_r.at[index],
            device_id={"req": partner},
        )

    def pair_landed(pos, slot, part):
        other = slot + 1 - 2 * core
        return pair_copy(pos, other, part)

    sent = []
    for way, part in ((0, 0), (1, 1), (0, 1), (1, 0)):
        copy = ring_copy(way, 0, part)
        copy.start()
        sent.append(copy)
    for part in range(2):
        copy = pair_copy(0, req, part)
        copy.start()
        sent.append(copy)

    def share(src_of, dst, send_sem, recv_sem):
        for n, peer in enumerate(peers):
            copy = pltpu.make_async_remote_copy(
                src_ref=src_of(peer), dst_ref=dst.at[mp],
                send_sem=send_sem.at[n], recv_sem=recv_sem.at[n],
                device_id={"mp": peer},
            )
            copy.start()
            sent.append(copy)

    def landed(n, src_of, dst, send_sem, recv_sem):
        pltpu.make_async_remote_copy(
            src_ref=src_of(peers[n]), dst_ref=dst.at[sources[n]],
            send_sem=send_sem.at[n], recv_sem=recv_sem.at[n],
            device_id={"mp": peers[n]},
        ).wait_recv()

    near_first = list(reversed(range(len(OFFSETS))))

    share(lambda peer: tok, xf, ag1_s, ag1_r)

    def service(hop):
        for way, part in ((0, 0), (1, 1), (0, 1), (1, 0)):
            if hop == 4 and way != part:
                continue
            ring_landed(way, hop, part).wait_recv()
            if hop < 3 or (hop == 3 and way == part):
                copy = ring_copy(way, hop, part)
                copy.start()
                sent.append(copy)
            slot = at_z(-hop) if way == 0 else at_z(hop)
            copy = pair_copy(hop if way == 0 else 4 + hop, slot, part)
            copy.start()
            sent.append(copy)

    starts = []
    total = jnp.int32(0)
    for r in range(4):
        starts.append(total)
        total = total + lengths[r, req]

    def meta(shape, axis):
        place = lax.broadcasted_iota(jnp.int32, shape, axis)
        request = jnp.zeros(shape, jnp.int32)
        start = jnp.zeros(shape, jnp.int32)
        group = jnp.full(shape, groups[0, req], jnp.int32)
        for r in range(1, 4):
            inside = place >= starts[r]
            request = request + inside.astype(jnp.int32)
            start = jnp.where(inside, starts[r], start)
            group = jnp.where(inside, groups[r, req], group)
        return place, request, place - start, group

    square = (128, 128)
    row_place, row_request, row_offset, row_group = meta(square, 0)
    col_place, col_request, _, _ = meta(square, 1)
    allowed = (row_request == col_request) & (col_place <= row_place)
    lane = lax.broadcasted_iota(jnp.int32, square, 1)
    in_head = lax.rem(lane, HEAD_DIM)
    pair = lax.rem(in_head, ROT // 2)
    frequency = jnp.zeros(square, F32)
    for i in range(ROT // 2):
        frequency = jnp.where(pair == i, F32(10000.0 ** (-(2.0 * i) / ROT)), frequency)
    angle = (PREFIX + row_offset).astype(F32) * frequency
    cosine, sine = jnp.cos(angle), jnp.sin(angle)
    lower = in_head < ROT // 2
    upper = (in_head >= ROT // 2) & (in_head < ROT)
    rot_same = jnp.where(in_head < ROT, cosine, 1.0)
    rot_up = jnp.where(lower, -sine, 0.0)
    rot_down = jnp.where(upper, sine, 0.0)

    def rotary(x):
        return (
            x * rot_same
            + pltpu.roll(x, 128 - ROT // 2, 1) * rot_up
            + pltpu.roll(x, ROT // 2, 1) * rot_down
        )

    service(1)

    def normalise(blocks, gain):
        total = jnp.zeros(square, F32)
        for j in range(N_MP):
            total = total + blocks[j].astype(F32)
        mean = jnp.sum(total, axis=1, keepdims=True) / (N_MP * 128)
        squares = jnp.zeros(square, F32)
        for j in range(N_MP):
            centred = blocks[j].astype(F32) - mean
            squares = squares + centred * centred
        scale = lax.rsqrt(jnp.sum(squares, axis=1, keepdims=True) / (N_MP * 128) + EPS)
        for j in range(N_MP):
            centred = blocks[j].astype(F32) - mean
            nrm[:, pl.ds(j * 128, 128)] = (
                centred * scale * gain[pl.ds(j, 1), :].astype(F32)
            ).astype(BF16)

    for n in near_first:
        landed(n, lambda peer: tok, xf, ag1_s, ag1_r)
    get_ga.wait()
    normalise(xf, gain_a)
    for copy in get_qkv:
        copy.wait()
    projected = dot(nrm[...], wqkv[...])
    query = rotary(projected[:, 0:128]).astype(BF16) * BF16(HEAD_DIM ** -0.5)
    keys = rotary(projected[:, 128:256]).astype(BF16)
    values = projected[:, 256:384].astype(BF16)

    zero = jnp.zeros(square, BF16)
    in_group = [(row_group == g) for g in range(2)]
    state = []
    for h in range(2):
        masked = jnp.where((lane // HEAD_DIM) == h, query, zero)
        for g in range(2):
            q2[pl.ds(h * 128, 128), pl.ds(g * 128, 128)] = jnp.where(in_group[g], masked, zero)
        scores = jnp.where(allowed, dot(masked, keys, ((1,), (1,))), NEG)
        top = jnp.max(scores, axis=1, keepdims=True)
        weights = jnp.exp(scores - top)
        mixed = dot(weights.astype(BF16), values)
        for g in range(2):
            acc[pl.ds(h * 128, 128), pl.ds(g * 128, 128)] = jnp.where(in_group[g], mixed, 0.0)
        state.append((top, jnp.sum(weights, axis=1, keepdims=True)))

    def attend(slots):
        for h in range(2):
            top, total = state[h]
            here = pl.ds(h * 128, 128)
            q = q2[here, :]
            scores = [dot(q, kv[slot, 0]) for slot in slots]
            best = functools.reduce(jnp.maximum, scores)
            new_top = jnp.maximum(top, jnp.max(best, axis=1, keepdims=True))
            scale = jnp.exp(top - new_top)
            weights = [jnp.exp(s - new_top) for s in scores]
            total = total * scale + jnp.sum(functools.reduce(jnp.add, weights), axis=1, keepdims=True)
            mixed = acc[here, :] * scale
            for w, slot in zip(weights, slots):
                mixed = mixed + dot(w.astype(BF16), kv[slot, 1])
            acc[here, :] = mixed
            state[h] = (new_top, total)

    def from_pair(pos, step, parts=(0, 1)):
        for part in parts:
            pair_landed(pos, at_z(step), part).wait_recv()

    def both(step):
        slot = at_z(step)
        return [slot, slot + 1 - 2 * core]

    from_pair(0, 0)
    attend(both(0))
    for hop in range(1, 4):
        service(hop + 1)
        from_pair(hop, -hop)
        from_pair(4 + hop, hop)
        attend(both(-hop) + both(hop))
    from_pair(4, -4, (0,))
    from_pair(8, 4, (1,))
    attend(both(4))

    finals = []
    for h in range(2):
        here = pl.ds(h * 128, 128)
        mixed = jnp.where(in_group[0], acc[here, pl.ds(0, 128)], acc[here, pl.ds(128, 128)])
        finals.append(mixed / state[h][1])
    attn_rows = jnp.where(lane < HEAD_DIM, finals[0], finals[1]).astype(BF16)

    get_out.wait()
    for j in range(N_MP // 2):
        share_pair = dot(attn_rows, wout[:, pl.ds(j * 256, 256)]).astype(BF16)
        p1s[2 * j] = share_pair[:, 0:128]
        p1s[2 * j + 1] = share_pair[:, 128:256]
    share(lambda peer: p1s.at[peer], p1r, rs1_s, rs1_r)
    attn_sum = p1s[mp].astype(F32)
    for n in near_first:
        landed(n, lambda peer: p1s.at[peer], p1r, rs1_s, rs1_r)
        attn_sum = attn_sum + p1r[sources[n]].astype(F32)
    residual = (tok[...].astype(F32) + attn_sum).astype(BF16)
    res[...] = residual
    rf[mp] = residual
    share(lambda peer: res, rf, ag2_s, ag2_r)
    get_gm.wait()
    get_gu.wait()
    get_down.wait()
    for n in near_first:
        landed(n, lambda peer: res, rf, ag2_s, ag2_r)

    normalise(rf, gain_m)
    gate_up = dot(wgu[...], nrm[...], ((1,), (1,)))
    units = wdown.shape[0]
    gate, up = gate_up[0:units], gate_up[units:]
    hidden = (gate / (1.0 + jnp.exp(-gate)) * up).astype(BF16)
    for j in range(N_MP // 2):
        share_pair = dot(hidden, wdown[:, pl.ds(j * 256, 256)], ((0,), (0,))).astype(BF16)
        p2s[2 * j] = share_pair[:, 0:128]
        p2s[2 * j + 1] = share_pair[:, 128:256]
    share(lambda peer: p2s.at[peer], p2r, rs2_s, rs2_r)
    mlp_sum = p2s[mp].astype(F32)
    for n in near_first:
        landed(n, lambda peer: p2s.at[peer], p2r, rs2_s, rs2_r)
        mlp_sum = mlp_sum + p2r[sources[n]].astype(F32)
    out_ref[...] = (res[...].astype(F32) + mlp_sum).astype(BF16)
    for copy in sent:
        copy.wait_send()


def body(
    tokens_in, req_lengths, req_groups, prefix_cache, attn_gain, mlp_gain, w_qkv, w_out, w_gate_up, w_down
):
    width = tokens_in.shape[1]
    model_width = w_qkv.shape[0]
    units = w_down.shape[0]
    rows = prefix_cache.shape[1]
    blocks = (N_MP, 128, 128)
    anywhere = pl.BlockSpec(memory_space=pl.ANY)
    scalars = pl.BlockSpec(memory_space=pltpu.SMEM)
    dma = pltpu.SemaphoreType.DMA
    return pl.pallas_call(
        layer_kernel,
        out_shape=jax.ShapeDtypeStruct(tokens_in.shape, BF16),
        in_specs=[scalars, scalars] + [anywhere] * 8,
        out_specs=pl.BlockSpec(memory_space=pltpu.VMEM),
        scratch_shapes=[
            pltpu.VMEM(tokens_in.shape, BF16),
            pltpu.VMEM((4 * rows, width), BF16),
            pltpu.VMEM((N_MP, 128), BF16),
            pltpu.VMEM((N_MP, 128), BF16),
            pltpu.VMEM((model_width, 384), BF16),
            pltpu.VMEM((width, model_width), BF16),
            pltpu.VMEM((2 * units, model_width), BF16),
            pltpu.VMEM((units, model_width), BF16),
            pltpu.VMEM(blocks, BF16),
            pltpu.VMEM((2 * N_Z, 2, rows, 256), BF16),
            pltpu.VMEM((128, model_width), BF16),
            pltpu.VMEM(blocks, BF16),
            pltpu.VMEM(blocks, BF16),
            pltpu.VMEM((128, 128), BF16),
            pltpu.VMEM(blocks, BF16),
            pltpu.VMEM(blocks, BF16),
            pltpu.VMEM(blocks, BF16),
            pltpu.VMEM((256, 256), BF16),
            pltpu.VMEM((256, 256), F32),
            dma((10,)),
        ]
        + [dma((15,))] * 8
        + [dma((16,)), dma((16,)), dma((18,)), dma((18,))],
        compiler_params=pltpu.CompilerParams(
            collective_id=0, has_side_effects=True, vmem_limit_bytes=60 * 1024 * 1024
        ),
        name="layer",
    )(
        req_lengths.T,
        req_groups.T,
        tokens_in,
        prefix_cache.reshape(4 * rows, width),
        attn_gain.reshape(N_MP, 128),
        mlp_gain.reshape(N_MP, 128),
        jnp.transpose(w_qkv, (1, 0, 2)),
        w_out,
        jnp.transpose(w_gate_up, (1, 2, 0)).reshape(2 * units, model_width),
        w_down,
    )


def solution(mesh):
    return jax.shard_map(
        body,
        mesh=mesh,
        in_specs=(
            P("req", "mp"),
            P(),
            P(),
            P(None, "req", None, "mp"),
            P(),
            P(),
            P(None, None, "mp"),
            P("mp", None),
            P(None, None, "mp"),
            P("mp", None),
        ),
        out_specs=P("req", "mp"),
        check_vma=False,
    )
```

```python
import functools

import jax
import jax.numpy as jnp
from jax import lax
from jax.experimental import pallas as pl
from jax.experimental.pallas import tpu as pltpu
from jax.sharding import PartitionSpec as P

HEAD_DIM = 64
ROT = 16
PREFIX = 4096
NEG = -1e30
EPS = 1e-05
F32 = jnp.float32
BF16 = jnp.bfloat16
N_MP = 16
N_Z = 8
SIDE = 4
HALF = 64
OFFSETS = sorted(
    [(dx, dy) for dx in range(SIDE) for dy in range(SIDE) if (dx, dy) != (0, 0)],
    key=lambda o: (-(min(o[0], SIDE - o[0]) + min(o[1], SIDE - o[1])), o),
)


def dot(a, b, dims=((1,), (0,))):
    return lax.dot_general(a, b, (dims, ((), ())), preferred_element_type=F32)


def layer_kernel(
    lengths, groups, tokens_hbm, prefix_hbm, gain_a_hbm, gain_m_hbm, wqkv_hbm, wout_hbm, wgu_hbm, wdown_hbm,
    out_ref,
    tok, pre, gain_a, gain_m, wqkv, wout, wgu, wdown,
    xf, kv, nrm, p1s, p1r, res, rf, p2s, p2r, q2, acc,
    local_sem, ag1_s, ag1_r, rs1_s, rs1_r, ag2_s, ag2_r, rs2_s, rs2_r, ring_s, ring_r, pair_s, pair_r,
):
    mp = lax.axis_index("mp")
    req = lax.axis_index("req")
    z, core = req // 2, req % 2
    mx, my = mp // SIDE, mp % SIDE

    def at_z(step):
        return lax.rem(z + (step + N_Z), N_Z) * 2 + core

    peers = [lax.rem(mx + dx, SIDE) * SIDE + lax.rem(my + dy, SIDE) for dx, dy in OFFSETS]
    sources = [
        lax.rem(mx + SIDE - dx, SIDE) * SIDE + lax.rem(my + SIDE - dy, SIDE) for dx, dy in OFFSETS
    ]
    right, left, partner = at_z(1), at_z(-1), z * 2 + (1 - core)

    barrier = pltpu.get_barrier_semaphore()
    for near in (right, left, partner):
        pl.semaphore_signal(barrier, inc=1, device_id={"req": near})
    for peer in peers:
        pl.semaphore_signal(barrier, inc=1, device_id={"mp": peer})

    def fetch(index, src, dst):
        copy = pltpu.make_async_copy(src, dst, local_sem.at[index])
        copy.start()
        return copy

    get_pre = fetch(0, prefix_hbm, pre)
    get_tok = fetch(1, tokens_hbm, tok)
    get_ga = fetch(2, gain_a_hbm, gain_a)
    get_gm = fetch(3, gain_m_hbm, gain_m)
    get_qkv = [
        fetch(4 + i, wqkv_hbm.at[i], wqkv.at[:, pl.ds(i * 128, 128)]) for i in range(3)
    ]
    get_out = fetch(7, wout_hbm, wout)
    get_gu = fetch(8, wgu_hbm, wgu)
    get_down = fetch(9, wdown_hbm, wdown)

    rows = kv.shape[2]
    get_pre.wait()
    pick_key = (
        lax.broadcasted_iota(jnp.int32, (2 * rows, rows), 0)
        == 2 * lax.broadcasted_iota(jnp.int32, (2 * rows, rows), 1)
    ).astype(F32).astype(BF16)
    pick_value = (
        lax.broadcasted_iota(jnp.int32, (rows, 2 * rows), 1)
        == 2 * lax.broadcasted_iota(jnp.int32, (rows, 2 * rows), 0) + 1
    ).astype(F32).astype(BF16)
    for g in range(2):
        raw = pre[pl.ds(g * 2 * rows, 2 * rows), :]
        kv[req, 0, pl.ds(g * 128, 128), :] = dot(raw, pick_key, ((0,), (0,))).astype(BF16)
        kv[req, 1, :, pl.ds(g * 128, 128)] = dot(pick_value, raw).astype(BF16)
    get_tok.wait()
    xf[mp] = tok[...]

    pl.semaphore_wait(barrier, 3 + len(OFFSETS))

    def ring_copy(way, hop, part):
        slot = at_z(-hop) if way == 0 else at_z(hop)
        index = way * 8 + hop * 2 + part
        return pltpu.make_async_remote_copy(
            src_ref=kv.at[slot, part], dst_ref=kv.at[slot, part],
            send_sem=ring_s.at[index], recv_sem=ring_r.at[index],
            device_id={"req": right if way == 0 else left},
        )

    def ring_landed(way, hop, part):
        slot = at_z(-hop) if way == 0 else at_z(hop)
        index = way * 8 + (hop - 1) * 2 + part
        return pltpu.make_async_remote_copy(
            src_ref=kv.at[slot, part], dst_ref=kv.at[slot, part],
            send_sem=ring_s.at[index], recv_sem=ring_r.at[index],
            device_id={"req": right if way == 0 else left},
        )

    def pair_copy(pos, slot, part):
        index = pos * 2 + part
        return pltpu.make_async_remote_copy(
            src_ref=kv.at[slot, part], dst_ref=kv.at[slot, part],
            send_sem=pair_s.at[index], recv_sem=pair_r.at[index],
            device_id={"req": partner},
        )

    def pair_landed(pos, slot, part):
        other = slot + 1 - 2 * core
        return pair_copy(pos, other, part)

    sent = []
    for way, part in ((0, 0), (1, 1), (0, 1), (1, 0)):
        copy = ring_copy(way, 0, part)
        copy.start()
        sent.append(copy)
    for part in range(2):
        copy = pair_copy(0, req, part)
        copy.start()
        sent.append(copy)

    def span(half):
        return pl.ds(half * HALF, HALF)

    def exchange(half, src_of, dst, send_sem, recv_sem, n):
        index = half * len(OFFSETS) + n
        return lambda peer, slot: pltpu.make_async_remote_copy(
            src_ref=src_of(peer).at[span(half)], dst_ref=dst.at[slot, span(half)],
            send_sem=send_sem.at[index], recv_sem=recv_sem.at[index],
            device_id={"mp": peer},
        )

    def share(half, src_of, dst, send_sem, recv_sem):
        for n, peer in enumerate(peers):
            copy = exchange(half, src_of, dst, send_sem, recv_sem, n)(peer, mp)
            copy.start()
            sent.append(copy)

    def landed(half, n, src_of, dst, send_sem, recv_sem):
        exchange(half, src_of, dst, send_sem, recv_sem, n)(peers[n], sources[n]).wait_recv()

    near_first = list(reversed(range(len(OFFSETS))))

    gather_in = (lambda peer: tok, xf, ag1_s, ag1_r)
    for half in range(2):
        share(half, *gather_in)

    def service(hop):
        for way, part in ((0, 0), (1, 1), (0, 1), (1, 0)):
            if hop == 4 and way != part:
                continue
            ring_landed(way, hop, part).wait_recv()
            if hop < 3 or (hop == 3 and way == part):
                copy = ring_copy(way, hop, part)
                copy.start()
                sent.append(copy)
            slot = at_z(-hop) if way == 0 else at_z(hop)
            copy = pair_copy(hop if way == 0 else 4 + hop, slot, part)
            copy.start()
            sent.append(copy)

    starts = []
    total = jnp.int32(0)
    for r in range(4):
        starts.append(total)
        total = total + lengths[r, req]

    def meta(shape, axis):
        place = lax.broadcasted_iota(jnp.int32, shape, axis)
        request = jnp.zeros(shape, jnp.int32)
        start = jnp.zeros(shape, jnp.int32)
        group = jnp.full(shape, groups[0, req], jnp.int32)
        for r in range(1, 4):
            inside = place >= starts[r]
            request = request + inside.astype(jnp.int32)
            start = jnp.where(inside, starts[r], start)
            group = jnp.where(inside, groups[r, req], group)
        return place, request, place - start, group

    square = (128, 128)
    row_place, row_request, row_offset, row_group = meta(square, 0)
    col_place, col_request, _, _ = meta(square, 1)
    allowed = (row_request == col_request) & (col_place <= row_place)
    lane = lax.broadcasted_iota(jnp.int32, square, 1)
    in_head = lax.rem(lane, HEAD_DIM)
    pair = lax.rem(in_head, ROT // 2)
    frequency = jnp.zeros(square, F32)
    for i in range(ROT // 2):
        frequency = jnp.where(pair == i, F32(10000.0 ** (-(2.0 * i) / ROT)), frequency)
    angle = (PREFIX + row_offset).astype(F32) * frequency
    cosine, sine = jnp.cos(angle), jnp.sin(angle)
    lower = in_head < ROT // 2
    upper = (in_head >= ROT // 2) & (in_head < ROT)
    rot_same = jnp.where(in_head < ROT, cosine, 1.0)
    rot_up = jnp.where(lower, -sine, 0.0)
    rot_down = jnp.where(upper, sine, 0.0)

    def rotary(x):
        return (
            x * rot_same
            + pltpu.roll(x, 128 - ROT // 2, 1) * rot_up
            + pltpu.roll(x, ROT // 2, 1) * rot_down
        )

    service(1)

    def normalise(blocks, gain, first, count):
        here = pl.ds(first, count)
        total = jnp.zeros((count, 128), F32)
        for j in range(N_MP):
            total = total + blocks[j, here].astype(F32)
        mean = jnp.sum(total, axis=1, keepdims=True) / (N_MP * 128)
        squares = jnp.zeros((count, 128), F32)
        for j in range(N_MP):
            centred = blocks[j, here].astype(F32) - mean
            squares = squares + centred * centred
        scale = lax.rsqrt(jnp.sum(squares, axis=1, keepdims=True) / (N_MP * 128) + EPS)
        for j in range(N_MP):
            centred = blocks[j, here].astype(F32) - mean
            nrm[here, pl.ds(j * 128, 128)] = (
                centred * scale * gain[pl.ds(j, 1), :].astype(F32)
            ).astype(BF16)

    for half in range(2):
        for n in near_first:
            landed(half, n, *gather_in)
    get_ga.wait()
    normalise(xf, gain_a, 0, 128)
    for copy in get_qkv:
        copy.wait()
    projected = dot(nrm[...], wqkv[...])
    query = rotary(projected[:, 0:128]).astype(BF16) * BF16(HEAD_DIM ** -0.5)
    keys = rotary(projected[:, 128:256]).astype(BF16)
    values = projected[:, 256:384].astype(BF16)

    zero = jnp.zeros(square, BF16)
    in_group = [(row_group == g) for g in range(2)]
    state = []
    for h in range(2):
        masked = jnp.where((lane // HEAD_DIM) == h, query, zero)
        for g in range(2):
            q2[pl.ds(h * 128, 128), pl.ds(g * 128, 128)] = jnp.where(in_group[g], masked, zero)
        scores = jnp.where(allowed, dot(masked, keys, ((1,), (1,))), NEG)
        top = jnp.max(scores, axis=1, keepdims=True)
        weights = jnp.exp(scores - top)
        mixed = dot(weights.astype(BF16), values)
        for g in range(2):
            acc[pl.ds(h * 128, 128), pl.ds(g * 128, 128)] = jnp.where(in_group[g], mixed, 0.0)
        state.append((top, jnp.sum(weights, axis=1, keepdims=True)))

    def attend(slots):
        for h in range(2):
            top, total = state[h]
            here = pl.ds(h * 128, 128)
            q = q2[here, :]
            scores = [dot(q, kv[slot, 0]) for slot in slots]
            best = functools.reduce(jnp.maximum, scores)
            new_top = jnp.maximum(top, jnp.max(best, axis=1, keepdims=True))
            scale = jnp.exp(top - new_top)
            weights = [jnp.exp(s - new_top) for s in scores]
            total = total * scale + jnp.sum(functools.reduce(jnp.add, weights), axis=1, keepdims=True)
            mixed = acc[here, :] * scale
            for w, slot in zip(weights, slots):
                mixed = mixed + dot(w.astype(BF16), kv[slot, 1])
            acc[here, :] = mixed
            state[h] = (new_top, total)

    def from_pair(pos, step, parts=(0, 1)):
        for part in parts:
            pair_landed(pos, at_z(step), part).wait_recv()

    def both(step):
        slot = at_z(step)
        return [slot, slot + 1 - 2 * core]

    from_pair(0, 0)
    attend(both(0))
    for hop in range(1, 4):
        service(hop + 1)
        from_pair(hop, -hop)
        from_pair(4 + hop, hop)
        attend(both(-hop) + both(hop))
    from_pair(4, -4, (0,))
    from_pair(8, 4, (1,))
    attend(both(4))

    finals = []
    for h in range(2):
        here = pl.ds(h * 128, 128)
        mixed = jnp.where(in_group[0], acc[here, pl.ds(0, 128)], acc[here, pl.ds(128, 128)])
        finals.append(mixed / state[h][1])
    attn_rows = jnp.where(lane < HEAD_DIM, finals[0], finals[1]).astype(BF16)

    scatter_attn = (lambda peer: p1s.at[peer], p1r, rs1_s, rs1_r)
    gather_mlp = (lambda peer: res, rf, ag2_s, ag2_r)
    scatter_mlp = (lambda peer: p2s.at[peer], p2r, rs2_s, rs2_r)

    def summed(half, own, exchange_of):
        total = own[mp, span(half)].astype(F32)
        for n in near_first:
            landed(half, n, *exchange_of)
            total = total + exchange_of[1][sources[n], span(half)].astype(F32)
        return total

    get_out.wait()
    for half in range(2):
        some_rows = attn_rows[half * HALF : (half + 1) * HALF]
        for j in range(N_MP // 2):
            share_pair = dot(some_rows, wout[:, pl.ds(j * 256, 256)]).astype(BF16)
            p1s[2 * j, span(half)] = share_pair[:, 0:128]
            p1s[2 * j + 1, span(half)] = share_pair[:, 128:256]
        share(half, *scatter_attn)
    get_gm.wait()
    get_gu.wait()
    get_down.wait()
    for half in range(2):
        attn_sum = summed(half, p1s, scatter_attn)
        residual = (tok[span(half)].astype(F32) + attn_sum).astype(BF16)
        res[span(half)] = residual
        rf[mp, span(half)] = residual
        share(half, *gather_mlp)

    units = wdown.shape[0]
    for half in range(2):
        for n in near_first:
            landed(half, n, *gather_mlp)
        normalise(rf, gain_m, half * HALF, HALF)
        gate_up = dot(wgu[...], nrm[span(half)], ((1,), (1,)))
        gate, up = gate_up[0:units], gate_up[units:]
        hidden = (gate / (1.0 + jnp.exp(-gate)) * up).astype(BF16)
        for j in range(N_MP // 2):
            share_pair = dot(hidden, wdown[:, pl.ds(j * 256, 256)], ((0,), (0,))).astype(BF16)
            p2s[2 * j, span(half)] = share_pair[:, 0:128]
            p2s[2 * j + 1, span(half)] = share_pair[:, 128:256]
        share(half, *scatter_mlp)
    for half in range(2):
        mlp_sum = summed(half, p2s, scatter_mlp)
        out_ref[span(half)] = (res[span(half)].astype(F32) + mlp_sum).astype(BF16)
    for copy in sent:
        copy.wait_send()


def body(
    tokens_in, req_lengths, req_groups, prefix_cache, attn_gain, mlp_gain, w_qkv, w_out, w_gate_up, w_down
):
    width = tokens_in.shape[1]
    model_width = w_qkv.shape[0]
    units = w_down.shape[0]
    rows = prefix_cache.shape[1]
    blocks = (N_MP, 128, 128)
    anywhere = pl.BlockSpec(memory_space=pl.ANY)
    scalars = pl.BlockSpec(memory_space=pltpu.SMEM)
    dma = pltpu.SemaphoreType.DMA
    return pl.pallas_call(
        layer_kernel,
        out_shape=jax.ShapeDtypeStruct(tokens_in.shape, BF16),
        in_specs=[scalars, scalars] + [anywhere] * 8,
        out_specs=pl.BlockSpec(memory_space=pltpu.VMEM),
        scratch_shapes=[
            pltpu.VMEM(tokens_in.shape, BF16),
            pltpu.VMEM((4 * rows, width), BF16),
            pltpu.VMEM((N_MP, 128), BF16),
            pltpu.VMEM((N_MP, 128), BF16),
            pltpu.VMEM((model_width, 384), BF16),
            pltpu.VMEM((width, model_width), BF16),
            pltpu.VMEM((2 * units, model_width), BF16),
            pltpu.VMEM((units, model_width), BF16),
            pltpu.VMEM(blocks, BF16),
            pltpu.VMEM((2 * N_Z, 2, rows, 256), BF16),
            pltpu.VMEM((128, model_width), BF16),
            pltpu.VMEM(blocks, BF16),
            pltpu.VMEM(blocks, BF16),
            pltpu.VMEM((128, 128), BF16),
            pltpu.VMEM(blocks, BF16),
            pltpu.VMEM(blocks, BF16),
            pltpu.VMEM(blocks, BF16),
            pltpu.VMEM((256, 256), BF16),
            pltpu.VMEM((256, 256), F32),
            dma((10,)),
        ]
        + [dma((30,))] * 8
        + [dma((16,)), dma((16,)), dma((18,)), dma((18,))],
        compiler_params=pltpu.CompilerParams(
            collective_id=0, has_side_effects=True, vmem_limit_bytes=60 * 1024 * 1024
        ),
        name="layer",
    )(
        req_lengths.T,
        req_groups.T,
        tokens_in,
        prefix_cache.reshape(4 * rows, width),
        attn_gain.reshape(N_MP, 128),
        mlp_gain.reshape(N_MP, 128),
        jnp.transpose(w_qkv, (1, 0, 2)),
        w_out,
        jnp.transpose(w_gate_up, (1, 2, 0)).reshape(2 * units, model_width),
        w_down,
    )


def solution(mesh):
    return jax.shard_map(
        body,
        mesh=mesh,
        in_specs=(
            P("req", "mp"),
            P(),
            P(),
            P(None, "req", None, "mp"),
            P(),
            P(),
            P(None, None, "mp"),
            P("mp", None),
            P(None, None, "mp"),
            P("mp", None),
        ),
        out_specs=P("req", "mp"),
        check_vma=False,
    )
```

```python
import functools

import jax
import jax.numpy as jnp
from jax import lax
from jax.experimental import pallas as pl
from jax.experimental.pallas import tpu as pltpu
from jax.sharding import PartitionSpec as P

HEAD_DIM = 64
ROT = 16
PREFIX = 4096
NEG = -1e30
EPS = 1e-05
F32 = jnp.float32
BF16 = jnp.bfloat16
N_MP = 16
N_Z = 8
SIDE = 4
HALF = 64
Z_STEPS = (4, 3, 5, 2, 6, 1, 7)
OFFSETS = sorted(
    [(dx, dy) for dx in range(SIDE) for dy in range(SIDE) if (dx, dy) != (0, 0)],
    key=lambda o: (-(min(o[0], SIDE - o[0]) + min(o[1], SIDE - o[1])), o),
)


def dot(a, b, dims=((1,), (0,))):
    return lax.dot_general(a, b, (dims, ((), ())), preferred_element_type=F32)


def layer_kernel(
    lengths, groups, tokens_hbm, prefix_hbm, gain_a_hbm, gain_m_hbm, wqkv_hbm, wout_hbm, wgu_hbm, wdown_hbm,
    out_ref,
    tok, pre, gain_a, gain_m, wqkv, wout, wgu, wdown,
    xf, kv, nrm, p1s, p1r, res, rf, p2s, p2r, qs, qr, po, pr, so, sr, flip,
    local_sem, ag1_s, ag1_r, rs1_s, rs1_r, ag2_s, ag2_r, rs2_s, rs2_r,
    q_s, q_r, part_s, part_r, stat_s, stat_r, pair_s, pair_r,
):
    mp = lax.axis_index("mp")
    req = lax.axis_index("req")
    z, core = req // 2, req % 2
    mx, my = mp // SIDE, mp % SIDE

    def z_at(step):
        return lax.rem(z + (step + N_Z), N_Z)

    peers = [lax.rem(mx + dx, SIDE) * SIDE + lax.rem(my + dy, SIDE) for dx, dy in OFFSETS]
    sources = [
        lax.rem(mx + SIDE - dx, SIDE) * SIDE + lax.rem(my + SIDE - dy, SIDE) for dx, dy in OFFSETS
    ]
    z_to = [z_at(step) for step in Z_STEPS]
    z_from = [z_at(-step) for step in Z_STEPS]
    partner = z * 2 + (1 - core)

    barrier = pltpu.get_barrier_semaphore()
    pl.semaphore_signal(barrier, inc=1, device_id={"req": partner})
    for there in z_to:
        pl.semaphore_signal(barrier, inc=1, device_id={"req": there * 2 + core})
    for peer in peers:
        pl.semaphore_signal(barrier, inc=1, device_id={"mp": peer})

    def fetch(index, src, dst):
        copy = pltpu.make_async_copy(src, dst, local_sem.at[index])
        copy.start()
        return copy

    get_pre = fetch(0, prefix_hbm, pre)
    get_tok = fetch(1, tokens_hbm, tok)
    get_ga = fetch(2, gain_a_hbm, gain_a)
    get_gm = fetch(3, gain_m_hbm, gain_m)
    get_qkv = [
        fetch(4 + i, wqkv_hbm.at[i], wqkv.at[:, pl.ds(i * 128, 128)]) for i in range(3)
    ]
    get_out = fetch(7, wout_hbm, wout)
    get_gu = fetch(8, wgu_hbm, wgu)
    get_down = fetch(9, wdown_hbm, wdown)

    rows = kv.shape[2]
    get_pre.wait()
    pick_key = (
        lax.broadcasted_iota(jnp.int32, (2 * rows, rows), 0)
        == 2 * lax.broadcasted_iota(jnp.int32, (2 * rows, rows), 1)
    ).astype(F32).astype(BF16)
    pick_value = (
        lax.broadcasted_iota(jnp.int32, (rows, 2 * rows), 1)
        == 2 * lax.broadcasted_iota(jnp.int32, (rows, 2 * rows), 0) + 1
    ).astype(F32).astype(BF16)
    for g in range(2):
        raw = pre[pl.ds(g * 2 * rows, 2 * rows), :]
        kv[core, 0, pl.ds(g * 128, 128), :] = dot(raw, pick_key, ((0,), (0,))).astype(BF16)
        kv[core, 1, :, pl.ds(g * 128, 128)] = dot(pick_value, raw).astype(BF16)
    get_tok.wait()
    xf[mp] = tok[...]

    pl.semaphore_wait(barrier, 1 + len(Z_STEPS) + len(OFFSETS))
    sent = []

    def span(half):
        return pl.ds(half * HALF, HALF)

    def exchange(half, src_of, dst, send_sem, recv_sem, n):
        index = half * len(OFFSETS) + n
        return lambda peer, slot: pltpu.make_async_remote_copy(
            src_ref=src_of(peer).at[span(half)], dst_ref=dst.at[slot, span(half)],
            send_sem=send_sem.at[index], recv_sem=recv_sem.at[index],
            device_id={"mp": peer},
        )

    def share(half, src_of, dst, send_sem, recv_sem):
        for n, peer in enumerate(peers):
            copy = exchange(half, src_of, dst, send_sem, recv_sem, n)(peer, mp)
            copy.start()
            sent.append(copy)

    def landed(half, n, src_of, dst, send_sem, recv_sem):
        exchange(half, src_of, dst, send_sem, recv_sem, n)(peers[n], sources[n]).wait_recv()

    near_first = list(reversed(range(len(OFFSETS))))

    gather_in = (lambda peer: tok, xf, ag1_s, ag1_r)
    for half in range(2):
        share(half, *gather_in)

    def pair_copy(slot):
        return pltpu.make_async_remote_copy(
            src_ref=kv.at[slot], dst_ref=kv.at[slot], send_sem=pair_s, recv_sem=pair_r,
            device_id={"req": partner},
        )

    to_partner = pair_copy(core)
    to_partner.start()
    sent.append(to_partner)

    def z_copy(half, n, src, dst, send_sem, recv_sem, there):
        index = half * len(Z_STEPS) + n
        return pltpu.make_async_remote_copy(
            src_ref=src, dst_ref=dst, send_sem=send_sem.at[index], recv_sem=recv_sem.at[index],
            device_id={"req": there * 2 + core},
        )

    def query_copy(half, n, slot):
        return z_copy(half, n, qs.at[span(half)], qr.at[slot, span(half)], q_s, q_r, z_to[n])

    def part_copy(half, n, slot, there):
        return z_copy(half, n, po.at[there, span(half)], pr.at[slot, span(half)], part_s, part_r, there)

    def stat_copy(half, n, slot, there):
        return z_copy(half, n, so.at[half, there], sr.at[half, slot], stat_s, stat_r, there)

    def meta(shape, axis, first, owner):
        place = lax.broadcasted_iota(jnp.int32, shape, axis) + first
        request = jnp.zeros(shape, jnp.int32)
        start = jnp.zeros(shape, jnp.int32)
        group = jnp.full(shape, groups[0, owner], jnp.int32)
        begin = jnp.int32(0)
        for r in range(1, 4):
            begin = begin + lengths[r - 1, owner]
            inside = place >= begin
            request = request + inside.astype(jnp.int32)
            start = jnp.where(inside, begin, start)
            group = jnp.where(inside, groups[r, owner], group)
        return place, request, place - start, group

    square = (128, 128)
    strip = (HALF, 128)
    row_offset = meta(square, 0, 0, req)[2]
    lane = lax.broadcasted_iota(jnp.int32, square, 1)
    in_head = lax.rem(lane, HEAD_DIM)
    turn = lax.rem(in_head, ROT // 2)
    frequency = jnp.zeros(square, F32)
    for i in range(ROT // 2):
        frequency = jnp.where(turn == i, F32(10000.0 ** (-(2.0 * i) / ROT)), frequency)
    angle = (PREFIX + row_offset).astype(F32) * frequency
    cosine, sine = jnp.cos(angle), jnp.sin(angle)
    lower = in_head < ROT // 2
    upper = (in_head >= ROT // 2) & (in_head < ROT)
    rot_same = jnp.where(in_head < ROT, cosine, 1.0)
    rot_up = jnp.where(lower, -sine, 0.0)
    rot_down = jnp.where(upper, sine, 0.0)
    strip_lane = lax.broadcasted_iota(jnp.int32, strip, 1)
    first_head = strip_lane < HEAD_DIM

    def rotary(x, half):
        here = slice(half * HALF, (half + 1) * HALF)
        return (
            x * rot_same[here]
            + pltpu.roll(x, 128 - ROT // 2, 1) * rot_up[here]
            + pltpu.roll(x, ROT // 2, 1) * rot_down[here]
        )

    def normalise(blocks, gain, first, count):
        here = pl.ds(first, count)
        total = jnp.zeros((count, 128), F32)
        for j in range(N_MP):
            total = total + blocks[j, here].astype(F32)
        mean = jnp.sum(total, axis=1, keepdims=True) / (N_MP * 128)
        squares = jnp.zeros((count, 128), F32)
        for j in range(N_MP):
            centred = blocks[j, here].astype(F32) - mean
            squares = squares + centred * centred
        scale = lax.rsqrt(jnp.sum(squares, axis=1, keepdims=True) / (N_MP * 128) + EPS)
        for j in range(N_MP):
            centred = blocks[j, here].astype(F32) - mean
            nrm[here, pl.ds(j * 128, 128)] = (
                centred * scale * gain[pl.ds(j, 1), :].astype(F32)
            ).astype(BF16)

    zero = jnp.zeros(strip, BF16)

    def split_heads(query):
        return [jnp.where(first_head, query, zero), jnp.where(first_head, zero, query)]

    def stat_rows(tops, sums):
        columns = jnp.zeros(strip, F32)
        for place, column in enumerate(tops + sums):
            columns = jnp.where(strip_lane == place, column, columns)
        turned = jnp.transpose(columns)[0:8]
        return jnp.concatenate([turned, turned], axis=1)

    def chip_part(half, query, owner):
        group = meta(strip, 0, half * HALF, owner)[3]
        wide = []
        for masked in split_heads(query):
            wide.append(
                jnp.concatenate(
                    [jnp.where(group == 0, masked, zero), jnp.where(group == 0, zero, masked)], axis=1
                )
            )
        wide = jnp.concatenate(wide, axis=0)
        scores = [dot(wide, kv[c, 0]) for c in range(2)]
        top = jnp.max(jnp.maximum(scores[0], scores[1]), axis=1, keepdims=True)
        weights = [jnp.exp(s - top) for s in scores]
        total = jnp.sum(weights[0] + weights[1], axis=1, keepdims=True)
        mixed = dot(weights[0].astype(BF16), kv[0, 1]) + dot(weights[1].astype(BF16), kv[1, 1])
        mixed = jnp.where(
            jnp.concatenate([group, group], axis=0) == 0, mixed[:, 0:128], mixed[:, 128:256]
        ) / total
        part = jnp.where(first_head, mixed[0:HALF], mixed[HALF:]).astype(BF16)
        return part, stat_rows([top[0:HALF], top[HALF:]], [total[0:HALF], total[HALF:]])

    def own_part(half, query, keys, values):
        count = keys.shape[0]
        shape = (HALF, count)
        place, request, _, _ = meta(shape, 0, half * HALF, req)
        key_place, key_request, _, _ = meta(shape, 1, 0, req)
        allowed = (request == key_request) & (key_place <= place)
        tops, sums, mixed = [], [], []
        for masked in split_heads(query):
            scores = jnp.where(allowed, dot(masked, keys, ((1,), (1,))), NEG)
            top = jnp.max(scores, axis=1, keepdims=True)
            weights = jnp.exp(scores - top)
            total = jnp.sum(weights, axis=1, keepdims=True)
            mixed.append(dot(weights.astype(BF16), values) / total)
            tops.append(top)
            sums.append(total)
        return jnp.where(first_head, mixed[0], mixed[1]), stat_rows(tops, sums)

    queries, keys, values = [], [], []
    for half in range(2):
        for n in near_first:
            landed(half, n, *gather_in)
        if half == 0:
            get_ga.wait()
            for copy in get_qkv:
                copy.wait()
        normalise(xf, gain_a, half * HALF, HALF)
        projected = dot(nrm[span(half)], wqkv[...])
        query = rotary(projected[:, 0:128], half).astype(BF16) * BF16(HEAD_DIM ** -0.5)
        qs[span(half)] = query
        for n in range(len(Z_STEPS)):
            copy = query_copy(half, n, z)
            copy.start()
            sent.append(copy)
        queries.append(query)
        keys.append(rotary(projected[:, 128:256], half).astype(BF16))
        values.append(projected[:, 256:384].astype(BF16))

    pair_copy(1 - core).wait_recv()
    own = [own_part(0, queries[0], keys[0], values[0])]
    own.append(own_part(1, queries[1], jnp.concatenate(keys, axis=0), jnp.concatenate(values, axis=0)))
    z_order = list(reversed(range(len(Z_STEPS))))
    for half in range(2):
        part, stat = chip_part(half, queries[half], req)
        pr[z, span(half)] = part
        sr[half, z] = stat
        for n in z_order:
            query_copy(half, n, z_from[n]).wait_recv()
            there = z_from[n]
            part, stat = chip_part(half, qr[there, span(half)], there * 2 + core)
            po[there, span(half)] = part
            so[half, there] = stat
            for copy in (stat_copy(half, n, z, there), part_copy(half, n, z, there)):
                copy.start()
                sent.append(copy)

    def attended(half):
        for n in range(len(Z_STEPS)):
            stat_copy(half, n, z_to[n], z_from[n]).wait_recv()
            part_copy(half, n, z_to[n], z_from[n]).wait_recv()
        stats = [sr[half, j] for j in range(N_Z)] + [own[half][1]]
        top = functools.reduce(jnp.maximum, stats)
        scaled = [jnp.exp(stat - top) * pltpu.roll(stat, 6, 0) for stat in stats]
        total = functools.reduce(jnp.add, scaled)
        total = jnp.where(lax.broadcasted_iota(jnp.int32, total.shape, 0) < 2, total, 1.0)
        for j, weight in enumerate(scaled):
            flip[pl.ds(j * 8, 8)] = weight / total
        columns = jnp.transpose(flip[...])[0:HALF]
        result = jnp.zeros(strip, F32)
        for j in range(N_Z + 1):
            part = own[half][0] if j == N_Z else pr[j, span(half)].astype(F32)
            weight = jnp.where(first_head, columns[:, j * 8 : j * 8 + 1], columns[:, j * 8 + 1 : j * 8 + 2])
            result = result + part * weight
        return result.astype(BF16)

    scatter_attn = (lambda peer: p1s.at[peer], p1r, rs1_s, rs1_r)
    gather_mlp = (lambda peer: res, rf, ag2_s, ag2_r)
    scatter_mlp = (lambda peer: p2s.at[peer], p2r, rs2_s, rs2_r)

    def summed(half, own, exchange_of):
        total = own[mp, span(half)].astype(F32)
        for n in near_first:
            landed(half, n, *exchange_of)
            total = total + exchange_of[1][sources[n], span(half)].astype(F32)
        return total

    get_out.wait()
    flip[...] = jnp.zeros_like(flip)
    for half in range(2):
        some_rows = attended(half)
        for j in range(N_MP // 2):
            share_pair = dot(some_rows, wout[:, pl.ds(j * 256, 256)]).astype(BF16)
            p1s[2 * j, span(half)] = share_pair[:, 0:128]
            p1s[2 * j + 1, span(half)] = share_pair[:, 128:256]
        share(half, *scatter_attn)
    get_gm.wait()
    get_gu.wait()
    get_down.wait()
    for half in range(2):
        attn_sum = summed(half, p1s, scatter_attn)
        residual = (tok[span(half)].astype(F32) + attn_sum).astype(BF16)
        res[span(half)] = residual
        rf[mp, span(half)] = residual
        share(half, *gather_mlp)

    units = wdown.shape[0]
    for half in range(2):
        for n in near_first:
            landed(half, n, *gather_mlp)
        normalise(rf, gain_m, half * HALF, HALF)
        gate_up = dot(wgu[...], nrm[span(half)], ((1,), (1,)))
        gate, up = gate_up[0:units], gate_up[units:]
        hidden = (gate / (1.0 + jnp.exp(-gate)) * up).astype(BF16)
        for j in range(N_MP // 2):
            share_pair = dot(hidden, wdown[:, pl.ds(j * 256, 256)], ((0,), (0,))).astype(BF16)
            p2s[2 * j, span(half)] = share_pair[:, 0:128]
            p2s[2 * j + 1, span(half)] = share_pair[:, 128:256]
        share(half, *scatter_mlp)
    for half in range(2):
        mlp_sum = summed(half, p2s, scatter_mlp)
        out_ref[span(half)] = (res[span(half)].astype(F32) + mlp_sum).astype(BF16)
    for copy in sent:
        copy.wait_send()


def body(
    tokens_in, req_lengths, req_groups, prefix_cache, attn_gain, mlp_gain, w_qkv, w_out, w_gate_up, w_down
):
    width = tokens_in.shape[1]
    model_width = w_qkv.shape[0]
    units = w_down.shape[0]
    rows = prefix_cache.shape[1]
    blocks = (N_MP, 128, 128)
    z_blocks = (N_Z, 128, 128)
    anywhere = pl.BlockSpec(memory_space=pl.ANY)
    scalars = pl.BlockSpec(memory_space=pltpu.SMEM)
    dma = pltpu.SemaphoreType.DMA
    return pl.pallas_call(
        layer_kernel,
        out_shape=jax.ShapeDtypeStruct(tokens_in.shape, BF16),
        in_specs=[scalars, scalars] + [anywhere] * 8,
        out_specs=pl.BlockSpec(memory_space=pltpu.VMEM),
        scratch_shapes=[
            pltpu.VMEM(tokens_in.shape, BF16),
            pltpu.VMEM((4 * rows, width), BF16),
            pltpu.VMEM((N_MP, 128), BF16),
            pltpu.VMEM((N_MP, 128), BF16),
            pltpu.VMEM((model_width, 384), BF16),
            pltpu.VMEM((width, model_width), BF16),
            pltpu.VMEM((2 * units, model_width), BF16),
            pltpu.VMEM((units, model_width), BF16),
            pltpu.VMEM(blocks, BF16),
            pltpu.VMEM((2, 2, rows, 256), BF16),
            pltpu.VMEM((128, model_width), BF16),
            pltpu.VMEM(blocks, BF16),
            pltpu.VMEM(blocks, BF16),
            pltpu.VMEM((128, 128), BF16),
            pltpu.VMEM(blocks, BF16),
            pltpu.VMEM(blocks, BF16),
            pltpu.VMEM(blocks, BF16),
            pltpu.VMEM((128, 128), BF16),
            pltpu.VMEM(z_blocks, BF16),
            pltpu.VMEM(z_blocks, BF16),
            pltpu.VMEM(z_blocks, BF16),
            pltpu.VMEM((2, N_Z, 8, 128), F32),
            pltpu.VMEM((2, N_Z, 8, 128), F32),
            pltpu.VMEM((128, 128), F32),
            dma((10,)),
        ]
        + [dma((30,))] * 8
        + [dma((14,))] * 6
        + [dma] * 2,
        compiler_params=pltpu.CompilerParams(
            collective_id=0, has_side_effects=True, vmem_limit_bytes=60 * 1024 * 1024
        ),
        name="layer",
    )(
        req_lengths.T,
        req_groups.T,
        tokens_in,
        prefix_cache.reshape(4 * rows, width),
        attn_gain.reshape(N_MP, 128),
        mlp_gain.reshape(N_MP, 128),
        jnp.transpose(w_qkv, (1, 0, 2)),
        w_out,
        jnp.transpose(w_gate_up, (1, 2, 0)).reshape(2 * units, model_width),
        w_down,
    )


def solution(mesh):
    return jax.shard_map(
        body,
        mesh=mesh,
        in_specs=(
            P("req", "mp"),
            P(),
            P(),
            P(None, "req", None, "mp"),
            P(),
            P(),
            P(None, None, "mp"),
            P("mp", None),
            P(None, None, "mp"),
            P("mp", None),
        ),
        out_specs=P("req", "mp"),
        check_vma=False,
    )
```
